128 devices in a mesh: dp: 16 (over z, y_hi, core), seq: 8 (over y_lo, x).
Axes of the slice: x: 4, y: 4 (y_hi: 2, y_lo: 2; y = y_hi * 2 + y_lo), z: 4, core: 2. Of those that a mesh axis runs over, the one named last changes fastest.
Arguments:
- tokens: bfloat16 [4096, 4096], P(('dp', 'seq')), may hold values from -6 to 6
- modality: int32 [4096], P(('dp', 'seq')), may hold values from 0 to 1, as said below
- gate_weight: bfloat16 [4096, 14336], P(None, 'dp'), may hold values from -0.09375 to 0.09375
- up_weight: bfloat16 [4096, 14336], P(None, 'dp'), may hold values from -0.09375 to 0.09375
- down_weight: bfloat16 [14336, 4096], P('dp'), may hold values from -0.046875 to 0.046875
- out_grad: bfloat16 [3072, 4096], P(('dp', 'seq')), may hold values from -1.5 to 1.5
Outputs:
- output: bfloat16 [3072, 4096], P(('dp', 'seq'))
- in_grad: bfloat16 [3072, 4096], P(('dp', 'seq'))
- gate_grad: bfloat16 [4096, 14336], P('seq', 'dp')
- up_grad: bfloat16 [4096, 14336], P('seq', 'dp')
- down_grad: bfloat16 [14336, 4096], P('dp', 'seq')
The draws below stay inside these ranges and needn't reach their ends.
Inputs may be any that keep to these rules, and one draw needn't show every extreme that they name: In each aligned block of 32 tokens (the tokens of one device) exactly 24 tokens have modality 1 (vision); all others have 0 (text).
All inputs are finite; a program needn't handle non-finite values.
Results may differ from the reference program's by a relative error of at most 0.014.
Values may be sent and summed in bfloat16 or wider, within the bound.
A program may use at most 128 MiB of HBM per device.

```python
import jax
import jax.numpy as jnp
from jax import lax

D = 4096
FF = 14336
TOK_DEV = 32
VIS_DEV = 24
TOKENS = 4096
VISION = 3072
N_DP = 16
N_SEQ = 8


def draw_modality(key, part):
    block_count = TOKENS // TOK_DEV
    block_keys = jax.random.split(key, block_count)

    def one_block(block_key):
        order = jax.random.permutation(block_key, TOK_DEV)
        return (order < VIS_DEV).astype(jnp.int32)
    return jax.vmap(one_block)(block_keys).reshape(TOKENS)


def levels(stream_key, dims, cuts, least, high):
    factor_of = 1.0
    for position, blocks in cuts:
        draws = jax.random.uniform(jax.random.fold_in(jax.random.fold_in(stream_key, 6), position), (blocks,), jnp.float32, least / len(cuts), high / len(cuts))
        factor_of = factor_of * jnp.repeat(jnp.exp(draws), dims[position] // blocks).reshape((-1,) + (1,) * (len(dims) - 1 - position))
    return factor_of


def scatter_about(key, extent, width, most, pieces=(), held_as=jnp.bfloat16):
    values = width * jax.random.normal(key, extent, jnp.float32)
    if pieces:
        values = values * levels(key, extent, pieces, -0.22, 0.18)
    return jnp.clip(values, -most, most).astype(held_as)


def setup_inputs(seed: int = 0) -> dict:
    arg_keys = jax.random.split(jax.random.key(seed), 7)
    tokens = scatter_about(arg_keys[0], (TOKENS, D), 1.0, 6.0, ((0, 128),))
    modality = draw_modality(jax.random.fold_in(arg_keys[6], 71), 0)
    gate_weight = scatter_about(arg_keys[2], (D, FF), D ** -0.5, 0.09375, ((1, 16),))
    up_weight = scatter_about(arg_keys[3], (D, FF), D ** -0.5, 0.09375, ((1, 16),))
    down_weight = scatter_about(arg_keys[4], (FF, D), FF ** -0.5, 0.046875, ((0, 16),))
    out_grad = scatter_about(arg_keys[5], (VISION, D), 0.25, 1.5, ((0, 128),))
    return dict(tokens=tokens, modality=modality, gate_weight=gate_weight, up_weight=up_weight, down_weight=down_weight, out_grad=out_grad)


def silu_parts(gate_proj):
    sigmoid_value = jax.nn.sigmoid(gate_proj)
    return gate_proj * sigmoid_value, sigmoid_value * (1.0 + gate_proj * (1.0 - sigmoid_value))


def rounded(partial_sum):
    narrow = lax.optimization_barrier(partial_sum.astype(jnp.bfloat16))
    return narrow.astype(jnp.float32)


def by_group(matrix, group):
    blocks = matrix.reshape(N_DP, N_SEQ, VIS_DEV, matrix.shape[1])
    return blocks[:, group].reshape(N_DP * VIS_DEV, matrix.shape[1])


def reference(tokens, modality, gate_weight, up_weight, down_weight, out_grad):
    where_vision = jnp.nonzero(modality == 1, size=VISION)[0].astype(jnp.int32)
    picked = tokens[where_vision]
    gate_proj = jnp.dot(picked, gate_weight, preferred_element_type=jnp.float32)
    up_proj = jnp.dot(picked, up_weight, preferred_element_type=jnp.float32)
    active, slope = silu_parts(gate_proj)
    hidden = (active * up_proj).astype(jnp.bfloat16)
    output = jnp.dot(hidden, down_weight, preferred_element_type=jnp.float32).astype(jnp.bfloat16)
    back_hidden = jnp.dot(out_grad, down_weight.T, preferred_element_type=jnp.float32)
    gate_back = (back_hidden * up_proj * slope).astype(jnp.bfloat16)
    up_back = (back_hidden * active).astype(jnp.bfloat16)
    in_grad = (jnp.dot(gate_back, gate_weight.T, preferred_element_type=jnp.float32)
               + jnp.dot(up_back, up_weight.T, preferred_element_type=jnp.float32)).astype(jnp.bfloat16)
    gate_total = jnp.zeros((D, FF), jnp.float32)
    up_total = jnp.zeros((D, FF), jnp.float32)
    down_total = jnp.zeros((FF, D), jnp.float32)
    for group in range(N_SEQ):
        group_in = by_group(picked, group)
        gate_total = gate_total + rounded(jnp.dot(group_in.T, by_group(gate_back, group), preferred_element_type=jnp.float32))
        up_total = up_total + rounded(jnp.dot(group_in.T, by_group(up_back, group), preferred_element_type=jnp.float32))
        down_total = down_total + rounded(jnp.dot(by_group(hidden, group).T, by_group(out_grad, group), preferred_element_type=jnp.float32))
    return (output, in_grad, gate_total.astype(jnp.bfloat16), up_total.astype(jnp.bfloat16), down_total.astype(jnp.bfloat16))
```

```python
import functools

import jax
import jax.numpy as jnp
from jax import lax
from jax.experimental import pallas as pl
from jax.experimental.pallas import tpu as pltpu
from jax.sharding import PartitionSpec as P

MESH = pl.DeviceIdType.MESH
BF16 = jnp.bfloat16
F32 = jnp.float32
ROWS = 48
GROUP = 384
W = 512
FS = 896
D = 4096
PIECES = 4
PIECE = FS // PIECES
SEMS = 176


def dot(a, b):
    return jnp.dot(a, b, preferred_element_type=F32)


def dot_cols(a, b):
    return lax.dot_general(a, b, (((1,), (1,)), ((), ())), preferred_element_type=F32)


def body(sel_ref, place_ref, tok_ref, cot_ref, wg_hbm, wu_hbm, wd_hbm, out_ref, grads_ref,
         wg, wu, wd, flat, cols, ht, swap_out, swap, core_in, z_in, y_in, hid, mid, grad_in,
         weight_sem, send_sem, recv_sem):
    dp, seq = lax.axis_index("dp"), lax.axis_index("seq")
    z, yh, c = dp // 4, (dp // 2) % 2, dp % 2
    yl, x = seq // 4, seq % 4

    def device(dz=0, dyh=0, dc=0, dyl=0, dx=0):
        return {
            "dp": ((z + dz) % 4) * 4 + ((yh + dyh) % 2) * 2 + (c + dc) % 2,
            "seq": ((yl + dyl) % 2) * 4 + (x + dx) % 4,
        }

    sibling = device(dc=1)
    far_y = device(dyh=1)
    near_y = device(dyl=1)
    z_at = {k: device(dz=k) for k in (1, 2, 3)}
    x_at = {k: device(dx=k) for k in (1, 2, 3)}

    loads = [
        pltpu.make_async_copy(s, d, weight_sem.at[i])
        for i, (s, d) in enumerate(((wg_hbm, wg), (wu_hbm, wu), (wd_hbm, wd)))
    ]
    for load in loads:
        load.start()

    barrier = pltpu.get_barrier_semaphore()
    peers = [sibling, far_y, near_y, *z_at.values(), *x_at.values()]
    for peer in peers:
        pl.semaphore_signal(barrier, inc=1, device_id=peer, device_id_type=MESH)

    count = [0]

    def send(src, dst, dev):
        i = count[0]
        count[0] += 1
        copy = pltpu.make_async_remote_copy(
            src_ref=src, dst_ref=dst, send_sem=send_sem.at[i], recv_sem=recv_sem.at[i],
            device_id=dev, device_id_type=MESH,
        )
        copy.start()
        return copy

    other = 1 - c

    def place(half, put):
        for t in range(4):
            at = pl.ds(pl.multiple_of((half * 4 + t) * W, W), W)
            put(1, t, dot(sel_ref[...], tok_ref[:, at]).astype(BF16))
            put(0, t, dot(place_ref[...], cot_ref[:, at]).astype(BF16))

    def put_other(a, t, value):
        swap_out[a, t] = value

    def put_own(a, t, value):
        flat[a, c, t, pl.ds(0, ROWS), :] = value

    place(other, put_other)
    place(c, put_own)

    pl.semaphore_wait(barrier, len(peers))

    def rows(q):
        return pl.ds(q * ROWS, ROWS)

    swaps = [send(swap_out.at[a], swap.at[a], sibling) for a in (1, 0)]

    class Gather:
        def __init__(self, chunk):
            self.chunk = chunk
            self.sent = []

        def put(self, q_src, q_dst, dev, half=None):
            copy = send(self.chunk(q_src, half), self.chunk(q_dst, half), dev)
            self.sent.append(copy)
            return copy

        def stage1(self):
            self.y = self.put(0, 1, far_y)
            self.right = self.put(0, 6, z_at[1])
            self.left = self.put(0, 2, z_at[3])
            self.sib = [self.put(0, 0, sibling)]

        def stage2(self):
            self.y.wait_recv()
            self.right_y = self.put(1, 7, z_at[1])
            self.left_y = self.put(1, 3, z_at[3])
            self.sib.append(self.put(1, 1, sibling))
            self.right.wait_recv()
            self.right2 = self.put(6, 4, z_at[1], 0)
            self.sib.append(self.put(6, 6, sibling))
            self.left.wait_recv()
            self.left2 = self.put(2, 4, z_at[3], 1)
            self.sib.append(self.put(2, 2, sibling))

        def stage3(self):
            self.right_y.wait_recv()
            self.right2_y = self.put(7, 5, z_at[1], 0)
            self.sib.append(self.put(7, 7, sibling))
            self.left_y.wait_recv()
            self.left2_y = self.put(3, 5, z_at[3], 1)
            self.sib.append(self.put(3, 3, sibling))

        def stage4(self):
            self.right2.wait_recv()
            self.left2.wait_recv()
            self.sib.append(self.put(4, 4, sibling))
            self.right2_y.wait_recv()
            self.left2_y.wait_recv()
            self.sib.append(self.put(5, 5, sibling))

        def finish(self):
            for copy in self.sib:
                copy.wait_recv()

        def sources_free(self):
            for copy in self.sent:
                copy.wait_send()

    def row_chunk(a):
        def chunk(q, half):
            if half is None:
                return flat.at[a, c, :, rows(q), :]
            return flat.at[a, c, :, rows(q), pl.ds(half * 256, 256)]
        return chunk

    def col_chunk(a):
        def chunk(q, half):
            lanes = pl.ds(0, W) if half is None else pl.ds(half * 256, 256)
            return cols.at[a, c, pl.ds(1, 3), rows(q), lanes]
        return chunk

    tok_rows, cot_rows = Gather(row_chunk(1)), Gather(row_chunk(0))
    tok_cols, cot_cols = Gather(col_chunk(1)), Gather(col_chunk(0))
    spread = {1: [], 0: []}

    def own_rows(a, copy):
        copy.wait_recv()
        for t in range(4):
            flat[a, c, t, rows(0), :] = flat[a, c, t, rows(0), :] + swap[a, t]

    def spread_cols(a):
        for e in (1, 3, 2):
            spread[a].append(
                send(flat.at[a, c, (x + e) % 4, rows(0), :], cols.at[a, c, 4 - e, rows(0), :], x_at[e])
            )

    own_rows(1, swaps[0])
    own_rows(0, swaps[1])
    tok_rows.stage1()
    spread_cols(1)
    spread_cols(0)
    tok_rows.stage2()
    cot_rows.stage1()
    tok_rows.stage3()
    tok_rows.stage4()
    tok_rows.finish()

    def project(weight, dst):
        def step(k, _):
            part = dot(flat[1, k // 4, k % 4], weight[pl.ds(pl.multiple_of(k * W, W), W), :])
            mid[dst] = mid[dst] + part
            return 0
        mid[dst] = jnp.zeros((GROUP, FS), F32)
        lax.fori_loop(0, 8, step, 0)

    loads[0].wait()
    project(wg, 0)
    cot_rows.stage2()
    loads[1].wait()
    project(wu, 1)

    def tiles(fn):
        for j in range(FS // 128):
            fn(pl.ds(j * 128, 128))

    def forward(at):
        gate, up = mid[0, :, at], mid[1, :, at]
        sig = jax.nn.sigmoid(gate)
        active = gate * sig
        value = active * up
        hid[0, :, at] = value.astype(BF16)
        ht[0, at, pl.ds(0, GROUP)] = value.T.astype(BF16)
        mid[0, :, at] = active
        mid[1, :, at] = up * (sig * (1.0 + gate * (1.0 - sig)))

    tiles(forward)

    def piece(m, p, d, half=None):
        if half is None:
            return ht.at[m, pl.ds(p * PIECE, PIECE), pl.ds(d * GROUP, GROUP)]
        return ht.at[m, pl.ds(p * PIECE + half * (PIECE // 2), PIECE // 2), pl.ds(d * GROUP, GROUP)]

    ring = {}
    ring2 = {}

    def ring_start(m):
        for p in range(PIECES):
            ring[m, p] = (send(piece(m, p, 0), piece(m, p, 3), x_at[1]), send(piece(m, p, 0), piece(m, p, 1), x_at[3]))

    def ring_pass(m, p):
        right, left = ring[m, p]
        right.wait_recv()
        a = send(piece(m, p, 3, 0), piece(m, p, 2, 0), x_at[1])
        left.wait_recv()
        b = send(piece(m, p, 1, 1), piece(m, p, 2, 1), x_at[3])
        ring2[m, p] = (a, b)

    ring_start(0)
    cot_rows.stage3()
    cot_rows.stage4()
    for copy in spread[0]:
        copy.wait_recv()
    cot_cols.stage1()
    cot_rows.finish()

    loads[2].wait()

    def back_step(k, _):
        part = dot_cols(flat[0, k // 4, k % 4], wd[:, pl.ds(pl.multiple_of(k * W, W), W)])
        hidden_back[...] = hidden_back[...] + part
        return 0

    hidden_back = mid.at[2]
    hidden_back[...] = jnp.zeros((GROUP, FS), F32)
    lax.fori_loop(0, 8, back_step, 0)
    cot_cols.stage2()

    def backward(at):
        back = mid[2, :, at]
        gate_back = back * mid[1, :, at]
        up_back = back * mid[0, :, at]
        hid[1, :, at] = gate_back.astype(BF16)
        hid[2, :, at] = up_back.astype(BF16)
        ht[1, at, pl.ds(0, GROUP)] = gate_back.T.astype(BF16)
        ht[2, at, pl.ds(0, GROUP)] = up_back.T.astype(BF16)

    tiles(backward)
    ring_start(1)
    ring_start(2)
    ring_pass(0, 0)
    cot_cols.stage3()
    ring_pass(0, 1)
    for copy in spread[1]:
        copy.wait_recv()
    tok_cols.stage1()
    cot_cols.stage4()

    for a in range(2):
        for h in range(2):
            cols[a, h, 0] = flat[a, h, x]
    for gather in (tok_rows, cot_rows):
        gather.sources_free()
    for a in range(2):
        for copy in spread[a]:
            copy.wait_send()

    def out_tile(h, t):
        k = h * 4 + t
        at = pl.ds(pl.multiple_of(k * W, W), W)
        flat[0, h, t] = dot(hid[0], wd[:, at]).astype(BF16)
        flat[1, h, t] = (dot_cols(hid[1], wg[at, :]) + dot_cols(hid[2], wu[at, :])).astype(BF16)

    def out_half(h):
        def step(t, _):
            out_tile(h, t)
            return 0
        lax.fori_loop(0, 4, step, 0)

    out_half(other)
    to_core = send(flat.at[:, other], core_in, sibling)
    ring_pass(0, 2)
    tok_cols.stage2()
    out_half(c)
    ring_pass(0, 3)
    tok_cols.stage3()
    cot_cols.finish()

    partner = {}

    def weight_grad(m, p):
        for copy in ring2[m, p]:
            copy.wait_recv()
        a = 0 if m == 0 else 1
        at = pl.ds(p * PIECE, PIECE)
        lhs = ht[m, at, :]
        theirs = wd.at[at, pl.ds(m * W, W)]
        theirs[...] = dot(lhs, cols[a, 1 - yl].reshape(4 * GROUP, W)).astype(BF16)
        partner[m, p] = send(theirs, grad_in.at[m, at, :], near_y)
        grads_ref[m, at, :] = dot(lhs, cols[a, yl].reshape(4 * GROUP, W)).astype(BF16)

    def weight_done(m, p):
        partner[m, p].wait_recv()
        at = pl.ds(p * PIECE, PIECE)
        grads_ref[m, at, :] = (grads_ref[m, at, :].astype(F32) + grad_in[m, at, :].astype(F32)).astype(BF16)

    weight_grad(0, 0)
    tok_cols.stage4()
    to_core.wait_recv()
    for a in range(2):
        for t in range(4):
            flat[a, c, t] = (flat[a, c, t].astype(F32) + core_in[a, t].astype(F32)).astype(BF16)
    to_z = {
        e: send(flat.at[:, c, :, pl.ds(e * 2 * ROWS, 2 * ROWS), :], z_in.at[e - 1], z_at[e]) for e in (1, 3, 2)
    }
    weight_grad(0, 1)
    weight_grad(0, 2)
    ring_pass(1, 0)
    weight_grad(0, 3)
    tok_cols.finish()

    order = [(m, p) for m in range(3) for p in range(PIECES)]
    finals = {}

    def z_done():
        for e in (1, 2, 3):
            to_z[e].wait_recv()
        for a in range(2):
            for t in range(4):
                total = flat[a, c, t, pl.ds(0, 2 * ROWS), :].astype(F32)
                for e in range(3):
                    total = total + z_in[e, a, t].astype(F32)
                flat[a, c, t, pl.ds(0, 2 * ROWS), :] = total.astype(BF16)
        finals["y"] = send(flat.at[:, c, :, rows(1), :], y_in, far_y)

    def y_done():
        finals["y"].wait_recv()
        for a in range(2):
            for t in range(4):
                out_ref[a, c, t] = (
                    flat[a, c, t, rows(0), :].astype(F32) + y_in[a, t].astype(F32)
                ).astype(BF16)
        finals["core"] = send(out_ref.at[:, c], out_ref.at[:, c], sibling)

    for i in range(4, 12):
        if i + 1 < 12:
            ring_pass(*order[i + 1])
        weight_grad(*order[i])
        weight_done(*order[i - 4])
        if i == 8:
            z_done()
        if i == 10:
            y_done()
    for i in range(8, 12):
        weight_done(*order[i])

    finals["core"].wait()
    for copy in swaps:
        copy.wait_send()
    finals["y"].wait_send()
    to_core.wait_send()
    for copy in to_z.values():
        copy.wait_send()
    for key in order:
        partner[key].wait_send()
        for copy in (*ring[key], *ring2[key]):
            copy.wait_send()
    for gather in (tok_cols, cot_cols):
        gather.sources_free()


def on_device(tokens, modality, gate_weight, up_weight, down_weight, out_grad):
    count = out_grad.shape[0]
    c = lax.axis_index("dp") % 2
    flags = modality == 1
    here = jnp.arange(tokens.shape[0], dtype=jnp.int32)
    ranks = jnp.sum((here[None, :] < here[:, None]) & flags[None, :], axis=1).astype(jnp.int32)
    slots = jnp.arange(2 * count, dtype=jnp.int32)[:, None] - c * count
    sel = ((ranks[None, :] == slots) & flags[None, :]).astype(BF16)
    place = (jnp.arange(count, dtype=jnp.int32)[None, :] == slots).astype(BF16)
    vmem, hbm = pl.BlockSpec(memory_space=pltpu.VMEM), pl.BlockSpec(memory_space=pltpu.HBM)
    out, grads = pl.pallas_call(
        body,
        out_shape=(
            jax.ShapeDtypeStruct((2, 2, 4, ROWS, W), BF16),
            jax.ShapeDtypeStruct((3, FS, W), BF16),
        ),
        in_specs=[vmem] * 4 + [hbm] * 3,
        out_specs=(vmem, vmem),
        scratch_shapes=[
            pltpu.VMEM((D, FS), BF16),
            pltpu.VMEM((D, FS), BF16),
            pltpu.VMEM((FS, D), BF16),
            pltpu.VMEM((2, 2, 4, GROUP, W), BF16),
            pltpu.VMEM((2, 2, 4, GROUP, W), BF16),
            pltpu.VMEM((3, FS, 4 * GROUP), BF16),
            pltpu.VMEM((2, 4, ROWS, W), BF16),
            pltpu.VMEM((2, 4, ROWS, W), BF16),
            pltpu.VMEM((2, 4, GROUP, W), BF16),
            pltpu.VMEM((3, 2, 4, 2 * ROWS, W), BF16),
            pltpu.VMEM((2, 4, ROWS, W), BF16),
            pltpu.VMEM((3, GROUP, FS), BF16),
            pltpu.VMEM((3, GROUP, FS), F32),
            pltpu.VMEM((3, FS, W), BF16),
            pltpu.SemaphoreType.DMA((3,)),
            pltpu.SemaphoreType.DMA((SEMS,)),
            pltpu.SemaphoreType.DMA((SEMS,)),
        ],
        compiler_params=pltpu.CompilerParams(
            collective_id=0, has_side_effects=True, vmem_limit_bytes=62 * 1024 * 1024
        ),
        name="ffn",
    )(sel, place, tokens, out_grad, gate_weight, up_weight, down_weight)
    rows = lax.dynamic_slice_in_dim(out, c * count, count, axis=3)
    rows = rows.transpose(0, 3, 1, 2, 4).reshape(2, count, D)
    return rows[0], rows[1], grads[1].T, grads[2].T, grads[0]


def solution(mesh):
    return jax.shard_map(
        on_device,
        mesh=mesh,
        in_specs=(
            P(("dp", "seq"), None),
            P(("dp", "seq")),
            P(None, "dp"),
            P(None, "dp"),
            P("dp", None),
            P(("dp", "seq"), None),
        ),
        out_specs=(
            P(("dp", "seq"), None),
            P(("dp", "seq"), None),
            P("seq", "dp"),
            P("seq", "dp"),
            P("dp", "seq"),
        ),
        check_vma=False,
    )
```

```python
import functools

import jax
import jax.numpy as jnp
from jax import lax
from jax.experimental import pallas as pl
from jax.experimental.pallas import tpu as pltpu
from jax.sharding import PartitionSpec as P

MESH = pl.DeviceIdType.MESH
BF16 = jnp.bfloat16
F32 = jnp.float32
ROWS = 48
GROUP = 384
W = 512
FS = 896
D = 4096
PIECES = ((0, 256), (256, 256), (512, 256), (768, 128))
SEMS = 176


def dot(a, b):
    return jnp.dot(a, b, preferred_element_type=F32)


def dot_cols(a, b):
    return lax.dot_general(a, b, (((1,), (1,)), ((), ())), preferred_element_type=F32)


def body(flag_ref, tok_ref, cot_ref, wg_hbm, wu_hbm, wd_hbm,
         out_ref, in_ref, gate_ref, up_ref, down_ref,
         wg, wu, wd, flat, cols, ht, swap, core_in, z_in, y_in, final, final_out, hid, mid, grad_in,
         weight_sem, send_sem, recv_sem):
    dp, seq = lax.axis_index("dp"), lax.axis_index("seq")
    z, yh, c = dp // 4, (dp // 2) % 2, dp % 2
    yl, x = seq // 4, seq % 4
    other = 1 - c

    def device(dz=0, dyh=0, dc=0, dyl=0, dx=0):
        return {
            "dp": ((z + dz) % 4) * 4 + ((yh + dyh) % 2) * 2 + (c + dc) % 2,
            "seq": ((yl + dyl) % 2) * 4 + (x + dx) % 4,
        }

    sibling = device(dc=1)
    far_y = device(dyh=1)
    near_y = device(dyl=1)
    z_at = {k: device(dz=k) for k in (1, 2, 3)}
    x_at = {k: device(dx=k) for k in (1, 2, 3)}

    loads = [
        pltpu.make_async_copy(s, d, weight_sem.at[i])
        for i, (s, d) in enumerate(((wg_hbm, wg), (wu_hbm, wu), (wd_hbm, wd)))
    ]
    for load in loads:
        load.start()

    barrier = pltpu.get_barrier_semaphore()
    peers = [sibling, far_y, near_y, *z_at.values(), *x_at.values()]
    for peer in peers:
        pl.semaphore_signal(barrier, inc=1, device_id=peer, device_id_type=MESH)

    count = [0]

    def send(src, dst, dev):
        i = count[0]
        count[0] += 1
        copy = pltpu.make_async_remote_copy(
            src_ref=src, dst_ref=dst, send_sem=send_sem.at[i], recv_sem=recv_sem.at[i],
            device_id=dev, device_id_type=MESH,
        )
        copy.start()
        return copy

    def rows(q):
        return pl.ds(q * ROWS, ROWS)

    tokens, cots = tok_ref.shape[0], cot_ref.shape[0]

    def grid(shape, dim):
        return lax.broadcasted_iota(jnp.int32, shape, dim)

    flags = (flag_ref[...] == 1).astype(F32)
    before = (grid((tokens, tokens), 0) < grid((tokens, tokens), 1)).astype(F32)
    ranks = dot(jnp.broadcast_to(flags, (8, tokens)), before)[0:1]
    slots = (grid((2 * cots, tokens), 0) - c * cots).astype(F32)
    sel = jnp.where(slots == ranks, flags, 0.0).astype(BF16)
    place_cots = (grid((2 * cots, cots), 0) - c * cots == grid((2 * cots, cots), 1)).astype(BF16)

    def place(a, half, put):
        for t in range(4):
            at = pl.ds(pl.multiple_of((half * 4 + t) * W, W), W)
            put(a, t, (dot(sel, tok_ref[:, at]) if a else dot(place_cots, cot_ref[:, at])).astype(BF16))

    def put_other(a, t, value):
        core_in[a, t, rows(0), :] = value

    def put_own(a, t, value):
        flat[a, c, t, rows(0), :] = value

    place(1, other, put_other)
    place(1, c, put_own)

    pl.semaphore_wait(barrier, len(peers))
    swaps = {1: send(core_in.at[1, :, rows(0), :], swap.at[1], sibling)}
    place(0, other, put_other)
    swaps[0] = send(core_in.at[0, :, rows(0), :], swap.at[0], sibling)
    place(0, c, put_own)
    class Gather:
        def __init__(self, chunk):
            self.chunk = chunk
            self.sent = []

        def put(self, q_src, q_dst, dev, half=None):
            copy = send(self.chunk(q_src, half), self.chunk(q_dst, half), dev)
            self.sent.append(copy)
            return copy

        def first_y(self):
            self.y = self.put(0, 1, far_y)
            self.sib = [self.put(0, 0, sibling)]

        def first_z(self):
            self.right = self.put(0, 6, z_at[1])
            self.left = self.put(0, 2, z_at[3])

        def stage2(self):
            self.right.wait_recv()
            self.right2 = self.put(6, 4, z_at[1], 0)
            self.over = [self.put(6, 7, far_y)]
            self.left.wait_recv()
            self.left2 = self.put(2, 4, z_at[3], 1)
            self.over.append(self.put(2, 3, far_y))
            self.sib += [self.put(6, 6, sibling), self.put(2, 2, sibling)]
            self.y.wait_recv()
            self.sib.append(self.put(1, 1, sibling))

        def stage3(self):
            self.right2.wait_recv()
            self.left2.wait_recv()
            self.over.append(self.put(4, 5, far_y))
            self.sib.append(self.put(4, 4, sibling))
            for copy, q in zip(self.over, (7, 3)):
                copy.wait_recv()
                self.sib.append(self.put(q, q, sibling))

        def stage4(self):
            self.over[2].wait_recv()
            self.sib.append(self.put(5, 5, sibling))

        def finish(self):
            for copy in self.sib:
                copy.wait_recv()

        def sources_free(self):
            for copy in self.sent:
                copy.wait_send()

    class GatherZ(Gather):
        def stage2(self):
            self.y.wait_recv()
            self.right_y = self.put(1, 7, z_at[1])
            self.left_y = self.put(1, 3, z_at[3])
            self.sib.append(self.put(1, 1, sibling))
            self.right.wait_recv()
            self.right2 = self.put(6, 4, z_at[1], 0)
            self.sib.append(self.put(6, 6, sibling))
            self.left.wait_recv()
            self.left2 = self.put(2, 4, z_at[3], 1)
            self.sib.append(self.put(2, 2, sibling))

        def stage3(self):
            self.right_y.wait_recv()
            self.right2_y = self.put(7, 5, z_at[1], 0)
            self.sib.append(self.put(7, 7, sibling))
            self.left_y.wait_recv()
            self.left2_y = self.put(3, 5, z_at[3], 1)
            self.sib.append(self.put(3, 3, sibling))

        def stage4(self):
            self.right2.wait_recv()
            self.left2.wait_recv()
            self.sib.append(self.put(4, 4, sibling))
            self.right2_y.wait_recv()
            self.left2_y.wait_recv()
            self.sib.append(self.put(5, 5, sibling))

    def row_chunk(a):
        def chunk(q, half):
            if half is None:
                return flat.at[a, c, :, rows(q), :]
            return flat.at[a, c, :, rows(q), pl.ds(half * 256, 256)]
        return chunk

    def col_chunk(a):
        def chunk(q, half):
            lanes = pl.ds(0, W) if half is None else pl.ds(half * 256, 256)
            return cols.at[a, c, pl.ds(1, 3), rows(q), lanes]
        return chunk

    tok_rows, cot_rows = GatherZ(row_chunk(1)), GatherZ(row_chunk(0))
    tok_cols, cot_cols = GatherZ(col_chunk(1)), GatherZ(col_chunk(0))
    spread = {1: [], 0: []}

    def own_rows(a):
        swaps[a].wait()
        for t in range(4):
            flat[a, c, t, rows(0), :] = flat[a, c, t, rows(0), :] + swap[a, t]

    def spread_cols(a):
        for e in (1, 3, 2):
            spread[a].append(
                send(flat.at[a, c, (x + e) % 4, rows(0), :], cols.at[a, c, 4 - e, rows(0), :], x_at[e])
            )

    def own_cols(a):
        for h in range(2):
            cols[a, h, 0] = flat[a, h, x]

    def rows_free(a, gather):
        gather.sources_free()
        for copy in spread[a]:
            copy.wait_send()

    def start_cols(a, gather):
        for copy in spread[a]:
            copy.wait_recv()
        gather.first_y()

    def project(weight, dst):
        def step(k, _):
            mid[dst] = mid[dst] + dot(flat[1, k // 4, k % 4], weight[pl.ds(pl.multiple_of(k * W, W), W), :])
            return 0
        mid[dst] = dot(flat[1, 0, 0], weight[pl.ds(0, W), :])
        lax.fori_loop(1, 8, step, 0)

    def project_back():
        def step(k, _):
            mid[2] = mid[2] + dot_cols(flat[0, k // 4, k % 4], wd[:, pl.ds(pl.multiple_of(k * W, W), W)])
            return 0
        mid[2] = dot_cols(flat[0, 0, 0], wd[:, pl.ds(0, W)])
        lax.fori_loop(1, 8, step, 0)

    def tiles(fn):
        for j in range(FS // 128):
            fn(pl.ds(j * 128, 128))

    def forward(at):
        gate, up = mid[0, :, at], mid[1, :, at]
        sig = jax.nn.sigmoid(gate)
        active = gate * sig
        value = active * up
        hid[0, :, at] = value.astype(BF16)
        ht[0, at, pl.ds(0, GROUP)] = value.T.astype(BF16)
        mid[0, :, at] = active
        mid[1, :, at] = up * (sig * (1.0 + gate * (1.0 - sig)))

    def backward(at):
        back = mid[2, :, at]
        gate_back = back * mid[1, :, at]
        up_back = back * mid[0, :, at]
        hid[1, :, at] = gate_back.astype(BF16)
        hid[2, :, at] = up_back.astype(BF16)
        ht[1, at, pl.ds(0, GROUP)] = gate_back.T.astype(BF16)
        ht[2, at, pl.ds(0, GROUP)] = up_back.T.astype(BF16)

    order = [(m, p) for m in range(3) for p in range(len(PIECES))]

    def piece(i, d, half=None):
        m, (start, size) = order[i][0], PIECES[order[i][1]]
        if half is not None:
            size //= 2
            start += half * size
        return ht.at[m, pl.ds(start, size), pl.ds(d * GROUP, GROUP)]

    ring, ring2, partner = {}, {}, {}

    def ring_start(i):
        ring[i] = (send(piece(i, 0), piece(i, 3), x_at[1]), send(piece(i, 0), piece(i, 1), x_at[3]))

    def ring_pass(i):
        right, left = ring[i]
        right.wait_recv()
        a = send(piece(i, 3, 0), piece(i, 2, 0), x_at[1])
        left.wait_recv()
        b = send(piece(i, 1, 1), piece(i, 2, 1), x_at[3])
        ring2[i] = (a, b)

    def parts(i):
        m, (start, size) = order[i][0], PIECES[order[i][1]]
        at = pl.ds(start, size)
        own = down_ref.at[at, :] if m == 0 else wd.at[at, pl.ds((3 + m) * W, W)]
        theirs = gate_ref.at[at, pl.ds(0, W)] if i == 0 else wd.at[at, pl.ds(m * W, W)]
        return m, at, theirs, own

    def weight_grad(i):
        for copy in ring2[i]:
            copy.wait_recv()
        m, at, theirs, own = parts(i)
        a = 0 if m == 0 else 1
        lhs = ht[m, at, :]
        theirs[...] = dot(lhs, cols[a, 1 - yl].reshape(4 * GROUP, W)).astype(BF16)
        partner[i] = send(theirs, grad_in.at[m, at, :], near_y)
        own[...] = dot(lhs, cols[a, yl].reshape(4 * GROUP, W)).astype(BF16)

    def weight_done(i):
        partner[i].wait()
        m, at, theirs, own = parts(i)
        total = own[...].astype(F32) + grad_in[m, at, :].astype(F32)
        if m == 0:
            down_ref[at, :] = total.astype(BF16)
        elif m == 1:
            gate_ref[:, at] = total.T.astype(BF16)
        else:
            up_ref[:, at] = total.T.astype(BF16)

    def out_half(h):
        def step(t, _):
            at = pl.ds(pl.multiple_of((h * 4 + t) * W, W), W)
            flat[1, h, t] = dot(hid[0], wd[:, at]).astype(BF16)
            return 0
        lax.fori_loop(0, 4, step, 0)

    def in_half(h):
        def step(t, _):
            at = pl.ds(pl.multiple_of((h * 4 + t) * W, W), W)
            flat[0, h, t] = (dot_cols(hid[1], wg[at, :]) + dot_cols(hid[2], wu[at, :])).astype(BF16)
            return 0
        lax.fori_loop(0, 4, step, 0)

    to_core, to_z, to_y, to_own = {}, {}, {}, {}

    def core_start(a):
        to_core[a] = send(flat.at[a, other], core_in.at[a], sibling)

    def core_done(a):
        to_core[a].wait_recv()
        for t in range(4):
            flat[a, c, t] = (flat[a, c, t].astype(F32) + core_in[a, t].astype(F32)).astype(BF16)
        to_z[a] = {
            e: send(flat.at[a, c, :, pl.ds(e * 2 * ROWS, 2 * ROWS), :], z_in.at[e - 1, a], z_at[e]) for e in (1, 3, 2)
        }

    def z_done(a):
        for e in (1, 2, 3):
            to_z[a][e].wait_recv()
        for t in range(4):
            total = flat[a, c, t, pl.ds(0, 2 * ROWS), :].astype(F32)
            for e in range(3):
                total = total + z_in[e, a, t].astype(F32)
            flat[a, c, t, pl.ds(0, 2 * ROWS), :] = total.astype(BF16)
        to_y[a] = send(flat.at[a, c, :, rows(1), :], y_in.at[a], far_y)

    def y_done(a):
        to_y[a].wait_recv()
        ref = out_ref if a else in_ref
        for t in range(4):
            final[...] = flat[a, c, t, rows(0), :].astype(F32) + y_in[a, t].astype(F32)
            at = pl.ds(pl.multiple_of((c * 4 + t) * W, W), W)
            ref[:, at] = final[pl.ds(pl.multiple_of(c * cots, 8), cots), :].astype(BF16)
            final_out[a, :, pl.ds(t * W, W)] = final[pl.ds(pl.multiple_of(other * cots, 8), cots), :].astype(BF16)
        half = pl.ds(pl.multiple_of(c * 4 * W, W), 4 * W)
        to_own[a] = send(final_out.at[a], ref.at[:, half], sibling)

    own_rows(1)
    tok_rows.first_y()
    tok_rows.first_z()
    spread_cols(1)
    own_rows(0)
    spread_cols(0)
    cot_rows.first_y()
    tok_rows.stage2()
    start_cols(0, cot_cols)
    tok_rows.stage3()
    cot_cols.first_z()
    tok_rows.stage4()
    cot_rows.first_z()
    tok_rows.finish()
    own_cols(1)
    loads[0].wait()
    project(wg, 0)
    cot_cols.stage2()
    loads[1].wait()
    project(wu, 1)
    tiles(forward)
    ring_start(0)
    ring_start(1)
    cot_rows.stage2()
    cot_cols.stage3()
    rows_free(1, tok_rows)
    loads[2].wait()
    out_half(other)
    core_start(1)
    ring_pass(0)
    ring_start(2)
    cot_rows.stage3()
    cot_cols.stage4()
    start_cols(1, tok_cols)
    tok_cols.first_z()
    ring_pass(1)
    ring_start(3)
    out_half(c)
    cot_rows.stage4()
    cot_rows.finish()
    own_cols(0)
    cot_cols.finish()
    ring_pass(2)
    tok_cols.stage2()
    weight_grad(0)
    project_back()
    tiles(backward)
    ring_start(4)
    ring_start(5)
    ring_pass(3)
    weight_grad(1)
    tok_cols.stage3()
    rows_free(0, cot_rows)
    in_half(other)
    core_start(0)
    weight_grad(2)
    ring_pass(4)
    ring_start(6)
    tok_cols.stage4()
    core_done(1)
    weight_grad(3)
    ring_pass(5)
    ring_start(7)
    tok_cols.finish()
    weight_grad(4)
    in_half(c)
    ring_pass(6)
    ring_start(8)
    weight_grad(5)
    core_done(0)
    ring_pass(7)
    ring_start(9)
    for i in range(6, 12):
        weight_grad(i)
        if i + 2 < 12:
            ring_pass(i + 2)
        if i + 4 < 12:
            ring_start(i + 4)
        weight_done(i - 6)
        if i == 6:
            z_done(1)
        if i == 8:
            y_done(1)
        if i == 9:
            z_done(0)
        if i == 11:
            y_done(0)
    for i in (6, 7):
        weight_done(i)
    for i in range(8, 12):
        weight_done(i)
    for a in (1, 0):
        to_own[a].wait()
        to_y[a].wait_send()
        to_core[a].wait_send()
        for copy in to_z[a].values():
            copy.wait_send()
    for i in range(12):
        for copy in (*ring[i], *ring2[i]):
            copy.wait_send()
    for gather in (tok_cols, cot_cols):
        gather.sources_free()


def store(*refs):
    held, sems = refs[10:15], refs[15]
    loads = [pltpu.make_async_copy(refs[i], held[i], sems.at[i]) for i in range(5)]
    stores = [pltpu.make_async_copy(held[i], refs[5 + i], sems.at[5 + i]) for i in range(5)]
    for copy in loads:
        copy.start()
    for load, copy in zip(loads, stores):
        load.wait()
        copy.start()
    for copy in stores:
        copy.wait()


def on_device(tokens, modality, gate_weight, up_weight, down_weight, out_grad):
    vmem, hbm = pl.BlockSpec(memory_space=pltpu.VMEM), pl.BlockSpec(memory_space=pltpu.HBM)
    count = out_grad.shape[0]
    out, in_grad, gate_grad, up_grad, down_grad = pl.pallas_call(
        body,
        out_shape=(
            jax.ShapeDtypeStruct((count, D), BF16),
            jax.ShapeDtypeStruct((count, D), BF16),
            jax.ShapeDtypeStruct((W, FS), BF16),
            jax.ShapeDtypeStruct((W, FS), BF16),
            jax.ShapeDtypeStruct((FS, W), BF16),
        ),
        in_specs=[vmem] * 3 + [hbm] * 3,
        out_specs=(vmem,) * 5,
        scratch_shapes=[
            pltpu.VMEM((D, FS), BF16),
            pltpu.VMEM((D, FS), BF16),
            pltpu.VMEM((FS, D), BF16),
            pltpu.VMEM((2, 2, 4, GROUP, W), BF16),
            pltpu.VMEM((2, 2, 4, GROUP, W), BF16),
            pltpu.VMEM((3, FS, 4 * GROUP), BF16),
            pltpu.VMEM((2, 4, ROWS, W), BF16),
            pltpu.VMEM((2, 4, GROUP, W), BF16),
            pltpu.VMEM((3, 2, 4, 2 * ROWS, W), BF16),
            pltpu.VMEM((2, 4, ROWS, W), BF16),
            pltpu.VMEM((ROWS, W), F32),
            pltpu.VMEM((2, ROWS // 2, 4 * W), BF16),
            pltpu.VMEM((3, GROUP, FS), BF16),
            pltpu.VMEM((3, GROUP, FS), F32),
            pltpu.VMEM((3, FS, W), BF16),
            pltpu.SemaphoreType.DMA((3,)),
            pltpu.SemaphoreType.DMA((SEMS,)),
            pltpu.SemaphoreType.DMA((SEMS,)),
        ],
        compiler_params=pltpu.CompilerParams(
            collective_id=0, has_side_effects=True, vmem_limit_bytes=62 * 1024 * 1024
        ),
        name="ffn",
    )(modality.reshape(1, -1), tokens, out_grad, gate_weight, up_weight, down_weight)
    results = (out, in_grad, gate_grad, up_grad, down_grad)
    return pl.pallas_call(
        store,
        out_shape=tuple(jax.ShapeDtypeStruct(r.shape, r.dtype) for r in results),
        in_specs=[hbm] * 5,
        out_specs=(hbm,) * 5,
        scratch_shapes=[pltpu.VMEM(r.shape, r.dtype) for r in results] + [pltpu.SemaphoreType.DMA((10,))],
        name="store",
    )(*results)


def solution(mesh):
    return jax.shard_map(
        on_device,
        mesh=mesh,
        in_specs=(
            P(("dp", "seq"), None),
            P(("dp", "seq")),
            P(None, "dp"),
            P(None, "dp"),
            P("dp", None),
            P(("dp", "seq"), None),
        ),
        out_specs=(
            P(("dp", "seq"), None),
            P(("dp", "seq"), None),
            P("seq", "dp"),
            P("seq", "dp"),
            P("dp", "seq"),
        ),
        check_vma=False,
    )
```

```python
import functools

import jax
import jax.numpy as jnp
from jax import lax
from jax.experimental import pallas as pl
from jax.experimental.pallas import tpu as pltpu
from jax.sharding import PartitionSpec as P

MESH = pl.DeviceIdType.MESH
BF16 = jnp.bfloat16
F32 = jnp.float32
ROWS = 48
GROUP = 384
W = 512
FS = 896
D = 4096
PIECES = ((0, 256), (256, 256), (512, 256), (768, 128))
SEMS = 176


def dot(a, b):
    return jnp.dot(a, b, preferred_element_type=F32)


def dot_cols(a, b):
    return lax.dot_general(a, b, (((1,), (1,)), ((), ())), preferred_element_type=F32)


def body(flag_ref, tok_ref, cot_ref, wg_hbm, wu_hbm, wd_hbm,
         out_ref, in_ref, gate_ref, up_ref, down_ref,
         wg, wu, wd, flat, cols, ht, swap, core_in, z_in, y_in, final, final_out, hid, mid, grad_in,
         weight_sem, send_sem, recv_sem):
    dp, seq = lax.axis_index("dp"), lax.axis_index("seq")
    z, yh, c = dp // 4, (dp // 2) % 2, dp % 2
    yl, x = seq // 4, seq % 4
    other = 1 - c

    def device(dz=0, dyh=0, dc=0, dyl=0, dx=0):
        return {
            "dp": ((z + dz) % 4) * 4 + ((yh + dyh) % 2) * 2 + (c + dc) % 2,
            "seq": ((yl + dyl) % 2) * 4 + (x + dx) % 4,
        }

    sibling = device(dc=1)
    far_y = device(dyh=1)
    near_y = device(dyl=1)
    z_at = {k: device(dz=k) for k in (1, 2, 3)}
    x_at = {k: device(dx=k) for k in (1, 2, 3)}

    loads = [
        pltpu.make_async_copy(s, d, weight_sem.at[i])
        for i, (s, d) in enumerate(((wg_hbm, wg), (wu_hbm, wu), (wd_hbm, wd)))
    ]
    for load in loads:
        load.start()

    barrier = pltpu.get_barrier_semaphore()
    peers = [sibling, far_y, near_y, *z_at.values(), *x_at.values()]
    for peer in peers:
        pl.semaphore_signal(barrier, inc=1, device_id=peer, device_id_type=MESH)

    count = [0]

    def send(src, dst, dev):
        i = count[0]
        count[0] += 1
        copy = pltpu.make_async_remote_copy(
            src_ref=src, dst_ref=dst, send_sem=send_sem.at[i], recv_sem=recv_sem.at[i],
            device_id=dev, device_id_type=MESH,
        )
        copy.start()
        return copy

    def rows(q):
        return pl.ds(q * ROWS, ROWS)

    tokens, cots = tok_ref.shape[0], cot_ref.shape[0]

    def grid(shape, dim):
        return lax.broadcasted_iota(jnp.int32, shape, dim)

    flags = (flag_ref[...] == 1).astype(F32)
    before = (grid((tokens, tokens), 0) < grid((tokens, tokens), 1)).astype(F32)
    ranks = dot(jnp.broadcast_to(flags, (8, tokens)), before)[0:1]
    slots = (grid((2 * cots, tokens), 0) - c * cots).astype(F32)
    sel = jnp.where(slots == ranks, flags, 0.0).astype(BF16)
    place_cots = (grid((2 * cots, cots), 0) - c * cots == grid((2 * cots, cots), 1)).astype(BF16)

    def place(a, half, put):
        for t in range(4):
            at = pl.ds(pl.multiple_of((half * 4 + t) * W, W), W)
            put(a, t, (dot(sel, tok_ref[:, at]) if a else dot(place_cots, cot_ref[:, at])).astype(BF16))

    def put_other(a, t, value):
        core_in[a, t, rows(0), :] = value

    def put_own(a, t, value):
        flat[a, c, t, rows(0), :] = value

    place(1, other, put_other)
    place(1, c, put_own)

    pl.semaphore_wait(barrier, len(peers))
    swaps = {1: send(core_in.at[1, :, rows(0), :], swap.at[1], sibling)}
    place(0, other, put_other)
    swaps[0] = send(core_in.at[0, :, rows(0), :], swap.at[0], sibling)
    place(0, c, put_own)
    class Gather:
        def __init__(self, chunk):
            self.chunk = chunk
            self.sent = []

        def put(self, q_src, q_dst, dev, half=None):
            copy = send(self.chunk(q_src, half), self.chunk(q_dst, half), dev)
            self.sent.append(copy)
            return copy

        def first_y(self):
            self.y = self.put(0, 1, far_y)
            self.sib = [self.put(0, 0, sibling)]

        def first_z(self):
            self.right = self.put(0, 6, z_at[1])
            self.left = self.put(0, 2, z_at[3])

        def stage2(self):
            self.right.wait_recv()
            self.right2 = self.put(6, 4, z_at[1], 0)
            self.over = [self.put(6, 7, far_y)]
            self.left.wait_recv()
            self.left2 = self.put(2, 4, z_at[3], 1)
            self.over.append(self.put(2, 3, far_y))
            self.sib += [self.put(6, 6, sibling), self.put(2, 2, sibling)]
            self.y.wait_recv()
            self.sib.append(self.put(1, 1, sibling))

        def stage3(self):
            self.right2.wait_recv()
            self.left2.wait_recv()
            self.over.append(self.put(4, 5, far_y))
            self.sib.append(self.put(4, 4, sibling))
            for copy, q in zip(self.over, (7, 3)):
                copy.wait_recv()
                self.sib.append(self.put(q, q, sibling))

        def stage4(self):
            self.over[2].wait_recv()
            self.sib.append(self.put(5, 5, sibling))

        def finish(self):
            for copy in self.sib:
                copy.wait_recv()

        def sources_free(self):
            for copy in self.sent:
                copy.wait_send()

    class GatherZ(Gather):
        def stage2(self):
            self.y.wait_recv()
            self.right_y = self.put(1, 7, z_at[1])
            self.left_y = self.put(1, 3, z_at[3])
            self.sib.append(self.put(1, 1, sibling))
            self.right.wait_recv()
            self.right2 = self.put(6, 4, z_at[1], 0)
            self.sib.append(self.put(6, 6, sibling))
            self.left.wait_recv()
            self.left2 = self.put(2, 4, z_at[3], 1)
            self.sib.append(self.put(2, 2, sibling))

        def stage3(self):
            self.right_y.wait_recv()
            self.right2_y = self.put(7, 5, z_at[1], 0)
            self.sib.append(self.put(7, 7, sibling))
            self.left_y.wait_recv()
            self.left2_y = self.put(3, 5, z_at[3], 1)
            self.sib.append(self.put(3, 3, sibling))

        def stage4(self):
            self.right2.wait_recv()
            self.left2.wait_recv()
            self.sib.append(self.put(4, 4, sibling))
            self.right2_y.wait_recv()
            self.left2_y.wait_recv()
            self.sib.append(self.put(5, 5, sibling))

    def row_chunk(a):
        def chunk(q, half):
            if half is None:
                return flat.at[a, c, :, rows(q), :]
            return flat.at[a, c, :, rows(q), pl.ds(half * 256, 256)]
        return chunk

    def col_chunk(a):
        def chunk(q, half):
            lanes = pl.ds(0, W) if half is None else pl.ds(half * 256, 256)
            return cols.at[a, c, pl.ds(1, 3), rows(q), lanes]
        return chunk

    tok_rows, cot_rows = GatherZ(row_chunk(1)), GatherZ(row_chunk(0))
    tok_cols, cot_cols = GatherZ(col_chunk(1)), GatherZ(col_chunk(0))
    spread = {1: [], 0: []}

    def own_rows(a):
        swaps[a].wait()
        for t in range(4):
            flat[a, c, t, rows(0), :] = flat[a, c, t, rows(0), :] + swap[a, t]

    def spread_cols(a):
        for e in (1, 3, 2):
            spread[a].append(
                send(flat.at[a, c, (x + e) % 4, rows(0), :], cols.at[a, c, 4 - e, rows(0), :], x_at[e])
            )

    def own_cols(a):
        for h in range(2):
            cols[a, h, 0] = flat[a, h, x]

    def rows_free(a, gather):
        gather.sources_free()
        for copy in spread[a]:
            copy.wait_send()

    def start_cols(a, gather):
        for copy in spread[a]:
            copy.wait_recv()
        gather.first_y()

    def project(weight, dst):
        def step(k, _):
            mid[dst] = mid[dst] + dot(flat[1, k // 4, k % 4], weight[pl.ds(pl.multiple_of(k * W, W), W), :])
            return 0
        mid[dst] = dot(flat[1, 0, 0], weight[pl.ds(0, W), :])
        lax.fori_loop(1, 8, step, 0)

    def project_gate():
        loads[0].wait()
        project(wg, 0)

    def project_up():
        loads[1].wait()
        project(wu, 1)

    def project_back():
        def step(k, _):
            mid[2] = mid[2] + dot_cols(flat[0, k // 4, k % 4], wd[:, pl.ds(pl.multiple_of(k * W, W), W)])
            return 0
        mid[2] = dot_cols(flat[0, 0, 0], wd[:, pl.ds(0, W)])
        lax.fori_loop(1, 8, step, 0)

    def tiles(fn):
        for j in range(FS // 128):
            fn(pl.ds(j * 128, 128))

    def forward(at):
        gate, up = mid[0, :, at], mid[1, :, at]
        sig = jax.nn.sigmoid(gate)
        active = gate * sig
        value = active * up
        hid[0, :, at] = value.astype(BF16)
        ht[0, at, pl.ds(0, GROUP)] = value.T.astype(BF16)
        mid[0, :, at] = active
        mid[1, :, at] = up * (sig * (1.0 + gate * (1.0 - sig)))

    def backward(at):
        back = mid[2, :, at]
        gate_back = back * mid[1, :, at]
        up_back = back * mid[0, :, at]
        hid[1, :, at] = gate_back.astype(BF16)
        hid[2, :, at] = up_back.astype(BF16)
        ht[1, at, pl.ds(0, GROUP)] = gate_back.T.astype(BF16)
        ht[2, at, pl.ds(0, GROUP)] = up_back.T.astype(BF16)

    order = [(m, p) for m in range(3) for p in range(len(PIECES))]

    def piece(i, d, half=None):
        m, (start, size) = order[i][0], PIECES[order[i][1]]
        if half is not None:
            size //= 2
            start += half * size
        return ht.at[m, pl.ds(start, size), pl.ds(d * GROUP, GROUP)]

    ring, ring2, partner = {}, {}, {}

    def ring_start(i):
        ring[i] = (send(piece(i, 0), piece(i, 3), x_at[1]), send(piece(i, 0), piece(i, 1), x_at[3]))

    def ring_pass(i):
        right, left = ring[i]
        right.wait_recv()
        a = send(piece(i, 3, 0), piece(i, 2, 0), x_at[1])
        left.wait_recv()
        b = send(piece(i, 1, 1), piece(i, 2, 1), x_at[3])
        ring2[i] = (a, b)

    def parts(i):
        m, (start, size) = order[i][0], PIECES[order[i][1]]
        at = pl.ds(start, size)
        own = down_ref.at[at, :] if m == 0 else wd.at[at, pl.ds((3 + m) * W, W)]
        theirs = gate_ref.at[at, pl.ds(0, W)] if i == 0 else wd.at[at, pl.ds(m * W, W)]
        return m, at, theirs, own

    def weight_grad(i):
        for copy in ring2[i]:
            copy.wait_recv()
        m, at, theirs, own = parts(i)
        a = 0 if m == 0 else 1
        lhs = ht[m, at, :]
        theirs[...] = dot(lhs, cols[a, 1 - yl].reshape(4 * GROUP, W)).astype(BF16)
        partner[i] = send(theirs, grad_in.at[m, at, :], near_y)
        own[...] = dot(lhs, cols[a, yl].reshape(4 * GROUP, W)).astype(BF16)

    def weight_done(i):
        partner[i].wait()
        m, at, theirs, own = parts(i)
        total = own[...].astype(F32) + grad_in[m, at, :].astype(F32)
        if m == 0:
            down_ref[at, :] = total.astype(BF16)
        elif m == 1:
            gate_ref[:, at] = total.T.astype(BF16)
        else:
            up_ref[:, at] = total.T.astype(BF16)

    def out_half(h):
        def step(t, _):
            at = pl.ds(pl.multiple_of((h * 4 + t) * W, W), W)
            flat[1, h, t] = dot(hid[0], wd[:, at]).astype(BF16)
            return 0
        lax.fori_loop(0, 4, step, 0)

    def in_half(h):
        def step(t, _):
            at = pl.ds(pl.multiple_of((h * 4 + t) * W, W), W)
            flat[0, h, t] = (dot_cols(hid[1], wg[at, :]) + dot_cols(hid[2], wu[at, :])).astype(BF16)
            return 0
        lax.fori_loop(0, 4, step, 0)

    to_core, to_z, to_y, to_own = {}, {}, {}, {}

    def core_start(a):
        to_core[a] = send(flat.at[a, other], core_in.at[a], sibling)

    def core_done(a):
        to_core[a].wait_recv()
        for t in range(4):
            flat[a, c, t] = (flat[a, c, t].astype(F32) + core_in[a, t].astype(F32)).astype(BF16)
        to_z[a] = {
            e: send(flat.at[a, c, :, pl.ds(e * 2 * ROWS, 2 * ROWS), :], z_in.at[e - 1, a], z_at[e]) for e in (1, 3, 2)
        }

    def z_done(a):
        for e in (1, 2, 3):
            to_z[a][e].wait_recv()
        for t in range(4):
            total = flat[a, c, t, pl.ds(0, 2 * ROWS), :].astype(F32)
            for e in range(3):
                total = total + z_in[e, a, t].astype(F32)
            flat[a, c, t, pl.ds(0, 2 * ROWS), :] = total.astype(BF16)
        to_y[a] = send(flat.at[a, c, :, rows(1), :], y_in.at[a], far_y)

    def y_done(a):
        to_y[a].wait_recv()
        ref = out_ref if a else in_ref
        for t in range(4):
            final[...] = flat[a, c, t, rows(0), :].astype(F32) + y_in[a, t].astype(F32)
            at = pl.ds(pl.multiple_of((c * 4 + t) * W, W), W)
            ref[:, at] = final[pl.ds(pl.multiple_of(c * cots, 8), cots), :].astype(BF16)
            final_out[a, :, pl.ds(t * W, W)] = final[pl.ds(pl.multiple_of(other * cots, 8), cots), :].astype(BF16)
        half = pl.ds(pl.multiple_of(c * 4 * W, W), 4 * W)
        to_own[a] = send(final_out.at[a], ref.at[:, half], sibling)

    def settle():
        for a in (1, 0):
            to_core[a].wait_send()
            for copy in to_z[a].values():
                copy.wait_send()
        for i in range(len(order)):
            for copy in (*ring[i], *ring2[i]):
                copy.wait_send()
        for gather in (tok_cols, cot_cols):
            gather.sources_free()

    own_rows(1)
    tok_rows.first_y()
    tok_rows.first_z()
    own_rows(0)
    cot_rows.first_y()
    spread_cols(0)
    tok_rows.stage2()
    start_cols(0, cot_cols)
    tok_rows.stage3()
    cot_rows.first_z()
    cot_cols.first_z()
    spread_cols(1)
    tok_rows.stage4()
    start_cols(1, tok_cols)
    tok_rows.finish()
    project_gate()
    cot_rows.stage2()
    project_up()
    tiles(forward)
    cot_rows.stage3()
    ring_start(0)
    cot_cols.stage2()
    ring_start(1)
    own_cols(1)
    rows_free(1, tok_rows)
    cot_rows.stage4()
    loads[2].wait()
    out_half(other)
    cot_rows.finish()
    ring_pass(0)
    cot_cols.stage3()
    ring_start(2)
    project_back()
    tok_cols.first_z()
    cot_cols.stage4()
    out_half(c)
    core_start(1)
    own_cols(0)
    ring_pass(1)
    cot_cols.finish()
    weight_grad(0)
    tok_cols.stage2()
    ring_start(3)
    ring_pass(2)
    tiles(backward)
    ring_start(4)
    weight_grad(1)
    tok_cols.stage3()
    rows_free(0, cot_rows)
    ring_pass(3)
    core_done(1)
    weight_grad(2)
    tok_cols.stage4()
    weight_done(0)
    ring_start(5)
    in_half(other)
    weight_done(1)
    ring_pass(4)
    weight_grad(3)
    core_start(0)
    ring_pass(5)
    ring_start(6)
    tok_cols.finish()
    weight_grad(4)
    in_half(c)
    weight_grad(5)
    core_done(0)
    ring_pass(6)
    weight_done(2)
    weight_done(3)
    ring_start(7)
    weight_done(4)
    z_done(1)
    ring_start(8)
    ring_pass(7)
    weight_grad(6)
    ring_start(9)
    ring_start(10)
    weight_grad(7)
    ring_pass(8)
    ring_pass(9)
    ring_start(11)
    weight_done(5)
    y_done(1)
    z_done(0)
    weight_grad(8)
    weight_grad(9)
    weight_done(6)
    weight_done(7)
    ring_pass(10)
    weight_grad(10)
    ring_pass(11)
    settle()
    weight_grad(11)
    weight_done(8)
    weight_done(9)
    y_done(0)
    weight_done(10)
    weight_done(11)
    for a in (1, 0):
        to_y[a].wait_send()
        to_own[a].wait()


def store(*refs):
    held, sems = refs[10:15], refs[15]
    loads = [pltpu.make_async_copy(refs[i], held[i], sems.at[i]) for i in range(5)]
    stores = [pltpu.make_async_copy(held[i], refs[5 + i], sems.at[5 + i]) for i in range(5)]
    for copy in loads:
        copy.start()
    for load, copy in zip(loads, stores):
        load.wait()
        copy.start()
    for copy in stores:
        copy.wait()


def on_device(tokens, modality, gate_weight, up_weight, down_weight, out_grad):
    vmem, hbm = pl.BlockSpec(memory_space=pltpu.VMEM), pl.BlockSpec(memory_space=pltpu.HBM)
    count = out_grad.shape[0]
    out, in_grad, gate_grad, up_grad, down_grad = pl.pallas_call(
        body,
        out_shape=(
            jax.ShapeDtypeStruct((count, D), BF16),
            jax.ShapeDtypeStruct((count, D), BF16),
            jax.ShapeDtypeStruct((W, FS), BF16),
            jax.ShapeDtypeStruct((W, FS), BF16),
            jax.ShapeDtypeStruct((FS, W), BF16),
        ),
        in_specs=[vmem] * 3 + [hbm] * 3,
        out_specs=(vmem,) * 5,
        scratch_shapes=[
            pltpu.VMEM((D, FS), BF16),
            pltpu.VMEM((D, FS), BF16),
            pltpu.VMEM((FS, D), BF16),
            pltpu.VMEM((2, 2, 4, GROUP, W), BF16),
            pltpu.VMEM((2, 2, 4, GROUP, W), BF16),
            pltpu.VMEM((3, FS, 4 * GROUP), BF16),
            pltpu.VMEM((2, 4, ROWS, W), BF16),
            pltpu.VMEM((2, 4, GROUP, W), BF16),
            pltpu.VMEM((3, 2, 4, 2 * ROWS, W), BF16),
            pltpu.VMEM((2, 4, ROWS, W), BF16),
            pltpu.VMEM((ROWS, W), F32),
            pltpu.VMEM((2, ROWS // 2, 4 * W), BF16),
            pltpu.VMEM((3, GROUP, FS), BF16),
            pltpu.VMEM((3, GROUP, FS), F32),
            pltpu.VMEM((3, FS, W), BF16),
            pltpu.SemaphoreType.DMA((3,)),
            pltpu.SemaphoreType.DMA((SEMS,)),
            pltpu.SemaphoreType.DMA((SEMS,)),
        ],
        compiler_params=pltpu.CompilerParams(
            collective_id=0, has_side_effects=True, vmem_limit_bytes=62 * 1024 * 1024
        ),
        name="ffn",
    )(modality.reshape(1, -1), tokens, out_grad, gate_weight, up_weight, down_weight)
    results = (out, in_grad, gate_grad, up_grad, down_grad)
    return pl.pallas_call(
        store,
        out_shape=tuple(jax.ShapeDtypeStruct(r.shape, r.dtype) for r in results),
        in_specs=[hbm] * 5,
        out_specs=(hbm,) * 5,
        scratch_shapes=[pltpu.VMEM(r.shape, r.dtype) for r in results] + [pltpu.SemaphoreType.DMA((10,))],
        name="store",
    )(*results)


def solution(mesh):
    return jax.shard_map(
        on_device,
        mesh=mesh,
        in_specs=(
            P(("dp", "seq"), None),
            P(("dp", "seq")),
            P(None, "dp"),
            P(None, "dp"),
            P("dp", None),
            P(("dp", "seq"), None),
        ),
        out_specs=(
            P(("dp", "seq"), None),
            P(("dp", "seq"), None),
            P("seq", "dp"),
            P("seq", "dp"),
            P("dp", "seq"),
        ),
        check_vma=False,
    )
```

```python
import functools

import jax
import jax.numpy as jnp
from jax import lax
from jax.experimental import pallas as pl
from jax.experimental.pallas import tpu as pltpu
from jax.sharding import PartitionSpec as P

MESH = pl.DeviceIdType.MESH
BF16 = jnp.bfloat16
F32 = jnp.float32
ROWS = 48
GROUP = 384
W = 512
FS = 896
D = 4096
PIECES = ((0, 256), (256, 256), (512, 256), (768, 128))
SEMS = 176


def dot(a, b):
    return jnp.dot(a, b, preferred_element_type=F32)


def dot_cols(a, b):
    return lax.dot_general(a, b, (((1,), (1,)), ((), ())), preferred_element_type=F32)


def body(flag_ref, tok_ref, cot_ref, wg_hbm, wu_hbm, wd_hbm,
         out_ref, in_ref, gate_ref, up_ref, down_ref,
         wg, wu, wd, flat, cols, ht, swap, core_in, z_in, y_in, final, final_out, hid, mid, grad_in,
         weight_sem, send_sem, recv_sem):
    dp, seq = lax.axis_index("dp"), lax.axis_index("seq")
    z, yh, c = dp // 4, (dp // 2) % 2, dp % 2
    yl, x = seq // 4, seq % 4
    other = 1 - c

    def device(dz=0, dyh=0, dc=0, dyl=0, dx=0):
        return {
            "dp": ((z + dz) % 4) * 4 + ((yh + dyh) % 2) * 2 + (c + dc) % 2,
            "seq": ((yl + dyl) % 2) * 4 + (x + dx) % 4,
        }

    sibling = device(dc=1)
    far_y = device(dyh=1)
    near_y = device(dyl=1)
    z_at = {k: device(dz=k) for k in (1, 2, 3)}
    x_at = {k: device(dx=k) for k in (1, 2, 3)}

    loads = [
        pltpu.make_async_copy(s, d, weight_sem.at[i])
        for i, (s, d) in enumerate(((wg_hbm, wg), (wu_hbm, wu), (wd_hbm, wd)))
    ]
    for load in loads:
        load.start()

    barrier = pltpu.get_barrier_semaphore()
    peers = [sibling, far_y, near_y, *z_at.values(), *x_at.values()]
    for peer in peers:
        pl.semaphore_signal(barrier, inc=1, device_id=peer, device_id_type=MESH)

    count = [0]

    def send(src, dst, dev):
        i = count[0]
        count[0] += 1
        copy = pltpu.make_async_remote_copy(
            src_ref=src, dst_ref=dst, send_sem=send_sem.at[i], recv_sem=recv_sem.at[i],
            device_id=dev, device_id_type=MESH,
        )
        copy.start()
        return copy

    def rows(q):
        return pl.ds(q * ROWS, ROWS)

    tokens, cots = tok_ref.shape[0], cot_ref.shape[0]

    def grid(shape, dim):
        return lax.broadcasted_iota(jnp.int32, shape, dim)

    flags = (flag_ref[...] == 1).astype(F32)
    before = (grid((tokens, tokens), 0) < grid((tokens, tokens), 1)).astype(F32)
    ranks = dot(jnp.broadcast_to(flags, (8, tokens)), before)[0:1]
    slots = (grid((2 * cots, tokens), 0) - c * cots).astype(F32)
    sel = jnp.where(slots == ranks, flags, 0.0).astype(BF16)
    place_cots = (grid((2 * cots, cots), 0) - c * cots == grid((2 * cots, cots), 1)).astype(BF16)

    def place(a, half, put):
        for t in range(4):
            at = pl.ds(pl.multiple_of((half * 4 + t) * W, W), W)
            put(a, t, (dot(sel, tok_ref[:, at]) if a else dot(place_cots, cot_ref[:, at])).astype(BF16))

    def put_other(a, t, value):
        core_in[a, t, rows(0), :] = value

    def put_own(a, t, value):
        flat[a, c, t, rows(0), :] = value

    place(1, other, put_other)
    place(1, c, put_own)

    pl.semaphore_wait(barrier, len(peers))
    swaps = {1: send(core_in.at[1, :, rows(0), :], swap.at[1], sibling)}
    place(0, other, put_other)
    swaps[0] = send(core_in.at[0, :, rows(0), :], swap.at[0], sibling)
    place(0, c, put_own)
    class Gather:
        def __init__(self, chunk):
            self.chunk = chunk
            self.sent = []

        def put(self, q_src, q_dst, dev, half=None):
            copy = send(self.chunk(q_src, half), self.chunk(q_dst, half), dev)
            self.sent.append(copy)
            return copy

        def first_y(self):
            self.y = self.put(0, 1, far_y)
            self.sib = [self.put(0, 0, sibling)]

        def first_z(self):
            self.right = self.put(0, 6, z_at[1])
            self.left = self.put(0, 2, z_at[3])

        def stage2(self):
            self.right.wait_recv()
            self.right2 = self.put(6, 4, z_at[1], 0)
            self.over = [self.put(6, 7, far_y)]
            self.left.wait_recv()
            self.left2 = self.put(2, 4, z_at[3], 1)
            self.over.append(self.put(2, 3, far_y))
            self.sib += [self.put(6, 6, sibling), self.put(2, 2, sibling)]
            self.y.wait_recv()
            self.sib.append(self.put(1, 1, sibling))

        def stage3(self):
            self.right2.wait_recv()
            self.left2.wait_recv()
            self.over.append(self.put(4, 5, far_y))
            self.sib.append(self.put(4, 4, sibling))
            for copy, q in zip(self.over, (7, 3)):
                copy.wait_recv()
                self.sib.append(self.put(q, q, sibling))

        def stage4(self):
            self.over[2].wait_recv()
            self.sib.append(self.put(5, 5, sibling))

        def finish(self):
            for copy in self.sib:
                copy.wait_recv()

        def sources_free(self):
            for copy in self.sent:
                copy.wait_send()

    class GatherZ(Gather):
        def stage2(self):
            self.y.wait_recv()
            self.right_y = self.put(1, 7, z_at[1])
            self.left_y = self.put(1, 3, z_at[3])
            self.sib.append(self.put(1, 1, sibling))
            self.right.wait_recv()
            self.right2 = self.put(6, 4, z_at[1], 0)
            self.sib.append(self.put(6, 6, sibling))
            self.left.wait_recv()
            self.left2 = self.put(2, 4, z_at[3], 1)
            self.sib.append(self.put(2, 2, sibling))

        def stage3(self):
            self.right_y.wait_recv()
            self.right2_y = self.put(7, 5, z_at[1], 0)
            self.sib.append(self.put(7, 7, sibling))
            self.left_y.wait_recv()
            self.left2_y = self.put(3, 5, z_at[3], 1)
            self.sib.append(self.put(3, 3, sibling))

        def stage4(self):
            self.right2.wait_recv()
            self.left2.wait_recv()
            self.sib.append(self.put(4, 4, sibling))
            self.right2_y.wait_recv()
            self.left2_y.wait_recv()
            self.sib.append(self.put(5, 5, sibling))

    def row_chunk(a):
        def chunk(q, half):
            if half is None:
                return flat.at[a, c, :, rows(q), :]
            return flat.at[a, c, :, rows(q), pl.ds(half * 256, 256)]
        return chunk

    def col_chunk(a):
        def chunk(q, half):
            lanes = pl.ds(0, W) if half is None else pl.ds(half * 256, 256)
            return cols.at[a, c, pl.ds(1, 3), rows(q), lanes]
        return chunk

    tok_rows, cot_rows = GatherZ(row_chunk(1)), Gather(row_chunk(0))
    tok_cols, cot_cols = GatherZ(col_chunk(1)), GatherZ(col_chunk(0))
    spread = {1: [], 0: []}

    def own_rows(a):
        swaps[a].wait()
        for t in range(4):
            flat[a, c, t, rows(0), :] = flat[a, c, t, rows(0), :] + swap[a, t]

    def spread_cols(a):
        for e in (1, 3, 2):
            spread[a].append(
                send(flat.at[a, c, (x + e) % 4, rows(0), :], cols.at[a, c, 4 - e, rows(0), :], x_at[e])
            )

    def own_cols(a):
        for h in range(2):
            cols[a, h, 0] = flat[a, h, x]

    def rows_free(a, gather):
        gather.sources_free()
        for copy in spread[a]:
            copy.wait_send()

    def start_cols(a, gather):
        for copy in spread[a]:
            copy.wait_recv()
        gather.first_y()

    def project(weight, dst):
        def step(k, _):
            mid[dst] = mid[dst] + dot(flat[1, k // 4, k % 4], weight[pl.ds(pl.multiple_of(k * W, W), W), :])
            return 0
        mid[dst] = dot(flat[1, 0, 0], weight[pl.ds(0, W), :])
        lax.fori_loop(1, 8, step, 0)

    def project_gate():
        loads[0].wait()
        project(wg, 0)

    def project_up():
        loads[1].wait()
        project(wu, 1)

    def project_back():
        def step(k, _):
            mid[2] = mid[2] + dot_cols(flat[0, k // 4, k % 4], wd[:, pl.ds(pl.multiple_of(k * W, W), W)])
            return 0
        mid[2] = dot_cols(flat[0, 0, 0], wd[:, pl.ds(0, W)])
        lax.fori_loop(1, 8, step, 0)

    def tiles(fn):
        for j in range(FS // 128):
            fn(pl.ds(j * 128, 128))

    def forward(at):
        gate, up = mid[0, :, at], mid[1, :, at]
        sig = jax.nn.sigmoid(gate)
        active = gate * sig
        value = active * up
        hid[0, :, at] = value.astype(BF16)
        ht[0, at, pl.ds(0, GROUP)] = value.T.astype(BF16)
        mid[0, :, at] = active
        mid[1, :, at] = up * (sig * (1.0 + gate * (1.0 - sig)))

    def backward(at):
        back = mid[2, :, at]
        gate_back = back * mid[1, :, at]
        up_back = back * mid[0, :, at]
        hid[1, :, at] = gate_back.astype(BF16)
        hid[2, :, at] = up_back.astype(BF16)
        ht[1, at, pl.ds(0, GROUP)] = gate_back.T.astype(BF16)
        ht[2, at, pl.ds(0, GROUP)] = up_back.T.astype(BF16)

    order = [(m, p) for m in range(3) for p in range(len(PIECES))]

    def piece(i, d, half=None):
        m, (start, size) = order[i][0], PIECES[order[i][1]]
        if half is not None:
            size //= 2
            start += half * size
        return ht.at[m, pl.ds(start, size), pl.ds(d * GROUP, GROUP)]

    ring, ring2, partner = {}, {}, {}

    def ring_start(i):
        ring[i] = (send(piece(i, 0), piece(i, 3), x_at[1]), send(piece(i, 0), piece(i, 1), x_at[3]))

    def ring_pass(i):
        right, left = ring[i]
        right.wait_recv()
        a = send(piece(i, 3, 0), piece(i, 2, 0), x_at[1])
        left.wait_recv()
        b = send(piece(i, 1, 1), piece(i, 2, 1), x_at[3])
        ring2[i] = (a, b)

    def parts(i):
        m, (start, size) = order[i][0], PIECES[order[i][1]]
        at = pl.ds(start, size)
        own = down_ref.at[at, :] if m == 0 else wd.at[at, pl.ds((3 + m) * W, W)]
        theirs = gate_ref.at[at, pl.ds(0, W)] if i == 0 else wd.at[at, pl.ds(m * W, W)]
        return m, at, theirs, own

    def weight_grad(i):
        for copy in ring2[i]:
            copy.wait_recv()
        m, at, theirs, own = parts(i)
        a = 0 if m == 0 else 1
        lhs = ht[m, at, :]
        theirs[...] = dot(lhs, cols[a, 1 - yl].reshape(4 * GROUP, W)).astype(BF16)
        partner[i] = send(theirs, grad_in.at[m, at, :], near_y)
        own[...] = dot(lhs, cols[a, yl].reshape(4 * GROUP, W)).astype(BF16)

    def weight_done(i):
        partner[i].wait()
        m, at, theirs, own = parts(i)
        total = own[...].astype(F32) + grad_in[m, at, :].astype(F32)
        if m == 0:
            down_ref[at, :] = total.astype(BF16)
        elif m == 1:
            gate_ref[:, at] = total.T.astype(BF16)
        else:
            up_ref[:, at] = total.T.astype(BF16)

    def out_half(h):
        def step(t, _):
            at = pl.ds(pl.multiple_of((h * 4 + t) * W, W), W)
            flat[1, h, t] = dot(hid[0], wd[:, at]).astype(BF16)
            return 0
        lax.fori_loop(0, 4, step, 0)

    def in_half(h):
        def step(t, _):
            at = pl.ds(pl.multiple_of((h * 4 + t) * W, W), W)
            flat[0, h, t] = (dot_cols(hid[1], wg[at, :]) + dot_cols(hid[2], wu[at, :])).astype(BF16)
            return 0
        lax.fori_loop(0, 4, step, 0)

    to_core, to_z, to_y, to_own = {}, {}, {}, {}

    def core_start(a):
        to_core[a] = send(flat.at[a, other], core_in.at[a], sibling)

    def core_done(a):
        to_core[a].wait_recv()
        for t in range(4):
            flat[a, c, t] = (flat[a, c, t].astype(F32) + core_in[a, t].astype(F32)).astype(BF16)
        to_z[a] = {
            e: send(flat.at[a, c, :, pl.ds(e * 2 * ROWS, 2 * ROWS), :], z_in.at[e - 1, a], z_at[e]) for e in (1, 3, 2)
        }

    def z_done(a):
        for e in (1, 2, 3):
            to_z[a][e].wait_recv()
        for t in range(4):
            total = flat[a, c, t, pl.ds(0, 2 * ROWS), :].astype(F32)
            for e in range(3):
                total = total + z_in[e, a, t].astype(F32)
            flat[a, c, t, pl.ds(0, 2 * ROWS), :] = total.astype(BF16)
        to_y[a] = send(flat.at[a, c, :, rows(1), :], y_in.at[a], far_y)

    def y_done(a):
        to_y[a].wait_recv()
        ref = out_ref if a else in_ref
        for t in range(4):
            final[...] = flat[a, c, t, rows(0), :].astype(F32) + y_in[a, t].astype(F32)
            at = pl.ds(pl.multiple_of((c * 4 + t) * W, W), W)
            ref[:, at] = final[pl.ds(pl.multiple_of(c * cots, 8), cots), :].astype(BF16)
            final_out[a, :, pl.ds(t * W, W)] = final[pl.ds(pl.multiple_of(other * cots, 8), cots), :].astype(BF16)
        half = pl.ds(pl.multiple_of(c * 4 * W, W), 4 * W)
        to_own[a] = send(final_out.at[a], ref.at[:, half], sibling)

    def settle():
        for a in (1, 0):
            to_core[a].wait_send()
            for copy in to_z[a].values():
                copy.wait_send()
        for i in range(len(order)):
            for copy in (*ring[i], *ring2[i]):
                copy.wait_send()
        for gather in (tok_cols, cot_cols):
            gather.sources_free()

    own_rows(1)
    tok_rows.first_z()
    tok_rows.first_y()
    own_rows(0)
    spread_cols(1)
    spread_cols(0)
    tok_rows.stage2()
    tok_rows.stage3()
    cot_rows.first_y()
    start_cols(0, cot_cols)
    start_cols(1, tok_cols)
    cot_rows.first_z()
    tok_rows.stage4()
    cot_cols.first_z()
    tok_rows.finish()
    project_gate()
    cot_rows.stage2()
    cot_cols.stage2()
    project_up()
    tiles(forward)
    tok_cols.first_z()
    ring_start(0)
    loads[2].wait()
    own_cols(1)
    cot_cols.stage3()
    cot_rows.stage3()
    ring_start(1)
    rows_free(1, tok_rows)
    out_half(c)
    out_half(other)
    cot_rows.stage4()
    ring_pass(0)
    tok_cols.stage2()
    cot_cols.stage4()
    ring_start(2)
    ring_start(3)
    core_start(1)
    cot_rows.finish()
    project_back()
    cot_cols.finish()
    own_cols(0)
    weight_grad(0)
    ring_pass(1)
    tiles(backward)
    ring_pass(2)
    ring_start(4)
    weight_grad(1)
    weight_done(0)
    tok_cols.stage3()
    core_done(1)
    ring_start(5)
    weight_grad(2)
    rows_free(0, cot_rows)
    ring_pass(3)
    tok_cols.stage4()
    ring_pass(4)
    in_half(other)
    weight_grad(3)
    ring_pass(5)
    core_start(0)
    tok_cols.finish()
    weight_grad(4)
    ring_start(6)
    in_half(c)
    ring_start(7)
    ring_start(8)
    weight_done(1)
    weight_grad(5)
    ring_pass(6)
    core_done(0)
    ring_pass(7)
    z_done(1)
    weight_done(2)
    ring_start(9)
    weight_done(3)
    weight_grad(6)
    ring_pass(8)
    weight_done(4)
    weight_done(5)
    ring_start(10)
    weight_grad(7)
    weight_grad(8)
    ring_start(11)
    z_done(0)
    ring_pass(9)
    ring_pass(10)
    weight_grad(9)
    weight_grad(10)
    ring_pass(11)
    y_done(1)
    weight_done(6)
    settle()
    weight_grad(11)
    weight_done(7)
    weight_done(8)
    y_done(0)
    weight_done(9)
    weight_done(10)
    weight_done(11)
    for a in (1, 0):
        to_y[a].wait_send()
        to_own[a].wait()


def store(*refs):
    held, sems = refs[10:15], refs[15]
    loads = [pltpu.make_async_copy(refs[i], held[i], sems.at[i]) for i in range(5)]
    stores = [pltpu.make_async_copy(held[i], refs[5 + i], sems.at[5 + i]) for i in range(5)]
    for copy in loads:
        copy.start()
    for load, copy in zip(loads, stores):
        load.wait()
        copy.start()
    for copy in stores:
        copy.wait()


def on_device(tokens, modality, gate_weight, up_weight, down_weight, out_grad):
    vmem, hbm = pl.BlockSpec(memory_space=pltpu.VMEM), pl.BlockSpec(memory_space=pltpu.HBM)
    count = out_grad.shape[0]
    out, in_grad, gate_grad, up_grad, down_grad = pl.pallas_call(
        body,
        out_shape=(
            jax.ShapeDtypeStruct((count, D), BF16),
            jax.ShapeDtypeStruct((count, D), BF16),
            jax.ShapeDtypeStruct((W, FS), BF16),
            jax.ShapeDtypeStruct((W, FS), BF16),
            jax.ShapeDtypeStruct((FS, W), BF16),
        ),
        in_specs=[vmem] * 3 + [hbm] * 3,
        out_specs=(vmem,) * 5,
        scratch_shapes=[
            pltpu.VMEM((D, FS), BF16),
            pltpu.VMEM((D, FS), BF16),
            pltpu.VMEM((FS, D), BF16),
            pltpu.VMEM((2, 2, 4, GROUP, W), BF16),
            pltpu.VMEM((2, 2, 4, GROUP, W), BF16),
            pltpu.VMEM((3, FS, 4 * GROUP), BF16),
            pltpu.VMEM((2, 4, ROWS, W), BF16),
            pltpu.VMEM((2, 4, GROUP, W), BF16),
            pltpu.VMEM((3, 2, 4, 2 * ROWS, W), BF16),
            pltpu.VMEM((2, 4, ROWS, W), BF16),
            pltpu.VMEM((ROWS, W), F32),
            pltpu.VMEM((2, ROWS // 2, 4 * W), BF16),
            pltpu.VMEM((3, GROUP, FS), BF16),
            pltpu.VMEM((3, GROUP, FS), F32),
            pltpu.VMEM((3, FS, W), BF16),
            pltpu.SemaphoreType.DMA((3,)),
            pltpu.SemaphoreType.DMA((SEMS,)),
            pltpu.SemaphoreType.DMA((SEMS,)),
        ],
        compiler_params=pltpu.CompilerParams(
            collective_id=0, has_side_effects=True, vmem_limit_bytes=62 * 1024 * 1024
        ),
        name="ffn",
    )(modality.reshape(1, -1), tokens, out_grad, gate_weight, up_weight, down_weight)
    results = (out, in_grad, gate_grad, up_grad, down_grad)
    return pl.pallas_call(
        store,
        out_shape=tuple(jax.ShapeDtypeStruct(r.shape, r.dtype) for r in results),
        in_specs=[hbm] * 5,
        out_specs=(hbm,) * 5,
        scratch_shapes=[pltpu.VMEM(r.shape, r.dtype) for r in results] + [pltpu.SemaphoreType.DMA((10,))],
        name="store",
    )(*results)


def solution(mesh):
    return jax.shard_map(
        on_device,
        mesh=mesh,
        in_specs=(
            P(("dp", "seq"), None),
            P(("dp", "seq")),
            P(None, "dp"),
            P(None, "dp"),
            P("dp", None),
            P(("dp", "seq"), None),
        ),
        out_specs=(
            P(("dp", "seq"), None),
            P(("dp", "seq"), None),
            P("seq", "dp"),
            P("seq", "dp"),
            P("dp", "seq"),
        ),
        check_vma=False,
    )
```
